32 devices in a mesh: blk: 16 (over z, x, core), head: 2 (over y).
Axes of the slice: x: 2, y: 2, z: 4, core: 2. Of those that a mesh axis runs over, the one named last changes fastest.
Arguments:
- query: bfloat16 [4096, 4096], P(('blk', 'head')), may hold values from -128 to 128
- key: bfloat16 [2048, 4096], P('blk', 'head'), may hold values from -8 to 8
- value: bfloat16 [2048, 4096], P('blk', 'head'), may hold values from -6 to 6
- d_out: bfloat16 [4096, 4096], P(('blk', 'head')), may hold values from -6 to 6
- seg_map: int32 [32], replicated, may hold values from 0 to 7, never falling along the last dimension, each value on 1 to 8 neighbouring positions
- spans: int32 [8, 8], replicated, may hold values from 0 to 15, all different within a row
Outputs:
- attn_out: bfloat16 [4096, 4096], P(('blk', 'head'))
- d_query: bfloat16 [4096, 4096], P(('blk', 'head'))
- d_key: bfloat16 [2048, 4096], P('blk', 'head')
- d_value: bfloat16 [2048, 4096], P('blk', 'head')
The draws below stay inside these ranges and needn't reach their ends.
Inputs may be any that keep to these rules, and one draw needn't show every extreme that they name: `seg_map`: segment numbers never fall from one CAD block to the next; each segment covers 1 to 8 blocks, one exactly 8. `spans`: each row names 8 different document blocks; every document block is named by some row.
All inputs are finite; a program needn't handle non-finite values.
Results may differ from the reference program's by a relative error of at most 0.024.
Values may be sent and summed in bfloat16 or wider, within the bound.
A program may use at most 128 MiB of HBM per device.

```python
import math
import jax
import jax.numpy as jnp
import numpy as np
from jax import lax

HEADS = 32
HEAD_DIM = 128
BLOCK = 128
SPANS = 8
CAD_TOK = 4096
DOC_TOK = 2048
ROWS_GROUP = 256
CAD_BLOCKS = 32
DOC_BLOCKS = 16
SEGS = 8
N_BLK = 16


def draw_query(key, part):
    sample = jax.random.normal(jax.random.fold_in(key, 1), (CAD_TOK, HEADS * HEAD_DIM), jnp.float32)
    sample = jnp.clip(sample, -6.0, 6.0)
    return sample.astype(jnp.bfloat16)


def draw_key(key, part):
    sample = jax.random.normal(jax.random.fold_in(key, 2), (DOC_TOK, HEADS * HEAD_DIM), jnp.float32)
    sample = jnp.clip(sample, -6.0, 6.0)
    return sample.astype(jnp.bfloat16)


def level_of(rng, dims, shards, low, largest):
    level, own = 1.0, jax.random.fold_in(rng, 6)
    for dim, blocks in shards:
        heights = jnp.exp(jax.random.uniform(jax.random.fold_in(own, dim), (blocks,), jnp.float32, low / len(shards), largest / len(shards)))
        level = level * jnp.repeat(heights, dims[dim] // blocks).reshape([-1 if axis == dim else 1 for axis in range(len(dims))])
    return level


def picks_of(own_key, rows, amount, top, lift):
    order = jax.random.permutation(jax.random.fold_in(own_key, 1), amount)
    boost = order
    for power in range(3):
        boost = boost * boost // amount
    boost = boost * lift // amount
    chance = jax.random.randint(jax.random.fold_in(own_key, 2), (rows, amount), 0, 4096) + boost
    fixed_rows = jax.random.permutation(jax.random.fold_in(own_key, 3), rows)[jnp.arange(amount) % rows]
    chance = jnp.where(jnp.arange(rows)[:, None] == fixed_rows[None, :], 1 << 14, chance)
    score = chance * amount + jnp.arange(amount)
    return lax.top_k(score.astype(jnp.int32), top)[1].astype(jnp.int32)


def split_up(amount, total, most, slope):
    portions = [(1 << 20) // math.isqrt(grade ** slope) + 1 for grade in range(2, amount + 1)]
    surplus, counts = total - most - (amount - 1), [1] * (amount - 1)
    while surplus > 0:
        candidates = [i for i in range(amount - 1) if counts[i] < most]
        mass, left = sum([portions[i] for i in candidates]), surplus
        for i in candidates:
            extra = min(most - counts[i], max(1, left * portions[i] // mass), surplus)
            counts[i] = counts[i] + extra
            surplus = surplus - extra
    return np.array([most] + counts)


def uneven(rng, number_of, total, most, skew):
    if number_of == 2:
        one = jax.random.randint(rng, (), max(1, total - most), min(most, total - 1) + 1)
        return jnp.stack([one, total - one])
    lengths = jnp.asarray(split_up(number_of, total, most, skew), jnp.int32)
    pairs = (number_of - 1) // 2
    source_of, taker = lengths[1:1 + 2 * pairs:2], lengths[2:2 + 2 * pairs:2]
    slack = jnp.minimum(source_of - 1, most - taker)
    moved = jax.random.randint(jax.random.fold_in(rng, 1), (pairs,), 0, 1 << 20) % (slack + 1)
    lengths = lengths.at[1:1 + 2 * pairs:2].set(source_of - moved).at[2:2 + 2 * pairs:2].set(taker + moved)
    return lengths[jax.random.permutation(jax.random.fold_in(rng, 2), number_of)]


def scatter_about(key, extent, scale, limit, shards=(), kind=jnp.bfloat16):
    loudness = level_of(key, extent, shards, -0.22, 0.18) if shards else 1.0
    values = jax.random.normal(key, extent, jnp.float32) * scale * loudness
    return jnp.minimum(jnp.maximum(values, -limit), limit).astype(kind)


def setup_inputs(seed: int = 0) -> dict:
    key_of = jax.random.split(jax.random.key(seed), 7)
    query = draw_query(jax.random.fold_in(key_of[6], 71), 0)
    key = draw_key(jax.random.fold_in(key_of[6], 71), 0)
    value = scatter_about(key_of[2], (DOC_TOK, HEADS * HEAD_DIM), 1.0, 6.0, ((0, 16), (1, 2)))
    d_out = scatter_about(key_of[3], (CAD_TOK, HEADS * HEAD_DIM), 1.0, 6.0, ((0, 32),))
    seg_map = jnp.searchsorted(jnp.cumsum(uneven(key_of[4], SEGS, CAD_BLOCKS, 8, 2)), jnp.arange(CAD_BLOCKS), side="right").astype(jnp.int32)
    spans = picks_of(key_of[5], SEGS, DOC_BLOCKS, SPANS, 8192)
    return {"query": query, "key": key, "value": value, "d_out": d_out, "seg_map": seg_map, "spans": spans}


def reference(query, key, value, d_out, seg_map, spans):
    factor = 1.0 / math.sqrt(HEAD_DIM)
    group_blocks = ROWS_GROUP // BLOCK
    all_width = HEADS * HEAD_DIM
    block_ids = spans[seg_map].astype(jnp.int32)
    key_blocks = key.reshape(DOC_BLOCKS, BLOCK, HEADS, HEAD_DIM)
    value_blocks = value.reshape(DOC_BLOCKS, BLOCK, HEADS, HEAD_DIM)

    def one_group(carry, inputs):
        query_group, dout_group, group_ids = inputs
        query_four = query_group.reshape(group_blocks, BLOCK, HEADS, HEAD_DIM).astype(jnp.float32)
        dout_four = dout_group.reshape(group_blocks, BLOCK, HEADS, HEAD_DIM).astype(jnp.float32)
        key_tiles = key_blocks[group_ids].reshape(group_blocks, SPANS * BLOCK, HEADS, HEAD_DIM).astype(jnp.float32)
        value_tiles = value_blocks[group_ids].reshape(group_blocks, SPANS * BLOCK, HEADS, HEAD_DIM).astype(jnp.float32)
        scores = jnp.einsum('cqhd,ckhd->chqk', query_four, key_tiles) * factor
        top_score = lax.optimization_barrier(jnp.max(scores, axis=-1, keepdims=True))
        expo = jnp.exp(scores - top_score)
        prob = expo / lax.optimization_barrier(jnp.sum(expo, axis=-1, keepdims=True))
        prob_b = prob.astype(jnp.bfloat16).astype(jnp.float32)
        attn = jnp.einsum('chqk,ckhd->cqhd', prob_b, value_tiles)
        delta = lax.optimization_barrier(jnp.sum(dout_four * attn, axis=-1))
        delta = jnp.transpose(delta, (0, 2, 1))[..., None]
        dprob = jnp.einsum('cqhd,ckhd->chqk', dout_four, value_tiles)
        dscore_b = (prob * (dprob - delta)).astype(jnp.bfloat16).astype(jnp.float32)
        grad_query = (jnp.einsum('chqk,ckhd->cqhd', dscore_b, key_tiles) * factor).astype(jnp.bfloat16)
        key_slots = jnp.einsum('chqk,cqhd->ckhd', dscore_b, query_four) * factor
        value_slots = jnp.einsum('chqk,cqhd->ckhd', prob_b, dout_four)
        flat_ids = group_ids.reshape(group_blocks * SPANS)
        key_sum = carry[0].at[flat_ids].add(key_slots.reshape(group_blocks * SPANS, BLOCK, all_width))
        value_sum = carry[1].at[flat_ids].add(value_slots.reshape(group_blocks * SPANS, BLOCK, all_width))
        outputs = (attn.astype(jnp.bfloat16).reshape(ROWS_GROUP, all_width), grad_query.reshape(ROWS_GROUP, all_width))
        return ((key_sum, value_sum), outputs)
    start_sums = (jnp.zeros((DOC_BLOCKS, BLOCK, all_width), jnp.float32), jnp.zeros((DOC_BLOCKS, BLOCK, all_width), jnp.float32))
    inputs = (query.reshape(N_BLK, ROWS_GROUP, all_width), d_out.reshape(N_BLK, ROWS_GROUP, all_width), block_ids.reshape(N_BLK, group_blocks, SPANS))
    (key_sum, value_sum), (attn_all, grad_all) = lax.scan(one_group, start_sums, inputs)
    attn_out = attn_all.reshape(CAD_TOK, all_width)
    d_query = grad_all.reshape(CAD_TOK, all_width)
    d_key = key_sum.reshape(DOC_TOK, all_width).astype(jnp.bfloat16)
    d_value = value_sum.reshape(DOC_TOK, all_width).astype(jnp.bfloat16)
    return (attn_out, d_query, d_key, d_value)
```

```python
import functools
import math

import jax
import jax.numpy as jnp
from jax import lax
from jax.experimental import pallas as pl
from jax.experimental.pallas import tpu as pltpu
from jax.sharding import PartitionSpec as P

HEADS = 32
HEAD_DIM = 128
BLOCK = 128
SPANS = 8
LOG2E = math.log2(math.e)

NT = (((1,), (1,)), ((), ()))
MESH = pl.DeviceIdType.MESH


def tile_sum(x, op):
    return op(x.reshape(x.shape[0] // 8, 8, x.shape[1]), axis=0)


def fused_kernel(
    blks, columns, factor,
    seg_ref, spans_ref, q_in, do_in, k_in, v_in,
    at_out, dq_out, dk_out, dv_out, dk_far, dv_far,
    q_s, do_s, k_s, v_s, kn, vn, kt, vt, p_s, ds_s, at_s, dq_s,
    xk_s, xv_s, xk_r, xv_r, dk_f, dv_f, dk_s, dv_s, s_ref, dp_ref, slot_ref,
    in_send, relay_send, x_send, out_send, far_send,
    k_recv, v_recv, kx_recv, vx_recv, q_recv, do_recv, xk_recv, xv_recv, out_recv,
):
    near = blks // 2
    lines = near // 2
    planes = blks // lines
    group = lines * columns
    members = near * columns
    share = HEADS // group
    docs = blks
    unroll, pair, chunk = 2, 2, 8
    blk, col = lax.axis_index("blk"), lax.axis_index("head")
    z, line = blk // lines, lax.rem(blk, lines)
    half = z // 2
    level = z - 2 * half
    place = line * columns + col
    mine = level * group + place
    inner = 1 - half
    is_inner = level == inner

    def inward(a_line):
        return share - 1 - lax.rem(a_line, 2)

    own = jnp.where(is_inner, inward(line), share - inward(line))

    def head_of(h):
        return line * share + jnp.where(is_inner, h, share - 1 - h)

    other = ((planes - 1 - z) * lines + line, col)
    bf16 = jnp.bfloat16

    def cols(index):
        return pl.ds(pl.multiple_of(index * HEAD_DIM, HEAD_DIM), HEAD_DIM)

    def member(m):
        return half * near + m // columns, lax.rem(m, columns)

    def turn(t, size):
        ahead = (t + 1) // 2
        back = lax.rem(t + 1, 2)
        return lax.rem(ahead + back * (size - 2 * ahead) + size, size)

    def local(src, dst, sem):
        pltpu.make_async_copy(src, dst, sem).start()

    def remote(src, dst, send, recv, where):
        pltpu.make_async_remote_copy(
            src_ref=src, dst_ref=dst, send_sem=send, recv_sem=recv,
            device_id=where, device_id_type=MESH,
        ).start()

    def wait_for(view, sem):
        pltpu.make_async_copy(view, view, sem).wait()

    barrier = pltpu.get_barrier_semaphore()

    @pl.loop(0, near)
    def _(t):
        to = ((1 - half) * near + t, col)
        pl.semaphore_signal(barrier, inc=1, device_id=to, device_id_type=MESH)

    @pl.loop(1, members)
    def _(t):
        to = member(lax.rem(mine + t, members))
        pl.semaphore_signal(barrier, inc=1, device_id=to, device_id_type=MESH)

    pl.semaphore_wait(barrier, near + members - 1)

    def place_of(j, to_line):
        inside = j < inward(to_line)
        return jnp.where(inside, inner, 1 - inner), jnp.where(inside, j, share - 1 - j)

    def send_docs(j):
        @pl.loop(0, lines)
        def _(t):
            to_line = lax.rem(line + t, lines)
            to_level, h = place_of(j, to_line)
            slot, at = h * docs + blk, h * 2 + level
            to = half * near + to_level * lines + to_line
            head = cols(to_line * share + j)

            @pl.when(to == blk)
            def _():
                local(k_in.at[:, head], k_s.at[slot], k_recv.at[at])
                local(v_in.at[:, head], v_s.at[slot], v_recv.at[at])

            @pl.when(to != blk)
            def _():
                remote(k_in.at[:, head], k_s.at[slot], in_send.at[0], k_recv.at[at], (to, col))
                remote(v_in.at[:, head], v_s.at[slot], in_send.at[1], v_recv.at[at], (to, col))

    def send_rows_in(j):
        @pl.loop(0, group)
        def _(t):
            spot = lax.rem(place + turn(t, group), group)
            to_line, to_col = spot // columns, lax.rem(spot, columns)
            to_level, h = place_of(j, to_line)
            slot = h * members + mine
            m = to_level * group + spot
            head = cols(to_col * (HEADS // columns) + to_line * share + j)

            @pl.when(m == mine)
            def _():
                local(q_in.at[:, head], q_s.at[slot], q_recv.at[slot])
                local(do_in.at[:, head], do_s.at[slot], do_recv.at[slot])

            @pl.when(m != mine)
            def _():
                remote(q_in.at[:, head], q_s.at[slot], in_send.at[2], q_recv.at[slot], member(m))
                remote(do_in.at[:, head], do_s.at[slot], in_send.at[3], do_recv.at[slot], member(m))

    def send_far(j):
        @pl.loop(0, lines)
        def _(t):
            to_line = lax.rem(line + t, lines)
            h = place_of(j, to_line)[1]
            inside = j < inward(to_line)
            to_z = jnp.where(inside, 2 - half, (planes - 1) * (1 - half))
            slot, at = h * docs + blk, h * 2 + level
            head = cols(to_line * share + j)
            to = (to_z * lines + to_line, col)

            @pl.when(jnp.logical_not(inside) | (is_inner & (j == 0)))
            def _():
                remote(k_in.at[:, head], k_s.at[slot], in_send.at[0], kx_recv.at[at], to)
                remote(v_in.at[:, head], v_s.at[slot], in_send.at[1], vx_recv.at[at], to)

    def relay(h, plane):
        at = h * 2 + plane
        rows = pl.ds(h * docs + half * near + plane * lines, lines)
        wait_for(k_s.at[rows], k_recv.at[at])
        remote(k_s.at[rows], k_s.at[rows], relay_send.at[0], kx_recv.at[at], other)
        wait_for(v_s.at[rows], v_recv.at[at])
        remote(v_s.at[rows], v_s.at[rows], relay_send.at[1], vx_recv.at[at], other)

    last = share - 1
    send_docs(0)

    @pl.when(is_inner)
    def _():
        send_far(0)

    send_docs(1)
    send_docs(last)
    send_rows_in(last)
    send_rows_in(0)

    @pl.when(is_inner)
    def _():
        relay(0, 1 - level)
        relay(1, level)
        relay(1, 1 - level)

    send_far(last)
    send_rows_in(1)
    for j in range(2, last):
        send_docs(j)
        send_far(j)
        send_rows_in(j)

    @pl.when(is_inner)
    def _():
        @pl.loop(2, own)
        def _(h):
            relay(h, level)

    @pl.loop(0, spans_ref.shape[0])
    def _(g):
        named = [spans_ref[g, j] for j in range(SPANS)]
        for d in range(docs):
            found = SPANS
            for j in range(SPANS):
                found = jnp.where(named[j] == d, j, found)
            slot_ref[g, d] = found

    @pl.loop(0, members)
    def _(m):
        p_s[m, SPANS] = jnp.zeros((BLOCK, BLOCK), bf16)
        ds_s[m, SPANS] = jnp.zeros((BLOCK, BLOCK), bf16)

    def source(t):
        far = t // group
        spot = lax.rem(place + group - turn(lax.rem(t, group), group), group)
        return lax.rem(level + far, 2) * group + spot

    def partial(h, first):
        ids = [first + u for u in range(pair)]
        outs = []
        for held, right, scale in ((ds_s, q_s, factor), (p_s, do_s, None)):
            total = jnp.zeros((pair * BLOCK, HEAD_DIM), jnp.float32)
            for i in range(0, members, chunk):
                segs = [seg_ref[half * members + i + c] for c in range(chunk)]
                left = jnp.concatenate([
                    jnp.concatenate([held[i + c, slot_ref[segs[c], d]] for c in range(chunk)], axis=1)
                    for d in ids], axis=0)
                rows = right[pl.ds(h * members + i, chunk)].reshape(chunk * BLOCK, HEAD_DIM)
                total = total + jnp.dot(left, rows, preferred_element_type=jnp.float32)
            if scale is not None:
                total = total * scale
            outs.append(total.reshape(pair, BLOCK, HEAD_DIM))
        return outs

    def send_sums(h, step, there):
        for u in range(pair):
            slot = h * near + step * pair + u
            to = half * near + step * pair + u

            @pl.when(to == blk)
            def _():
                local(dk_s.at[slot], dk_out.at[:, there], out_recv.at[2])
                local(dv_s.at[slot], dv_out.at[:, there], out_recv.at[3])

            @pl.when(to != blk)
            def _():
                remote(dk_s.at[slot], dk_out.at[:, there], out_send.at[2], out_recv.at[2], (to, col))
                remote(dv_s.at[slot], dv_out.at[:, there], out_send.at[3], out_recv.at[3], (to, col))

    def finalize(h):
        there = cols(head_of(h))

        @pl.loop(0, near // pair)
        def _(step):
            at = h * (near // pair) + step
            rows = pl.ds(h * near + step * pair, pair)
            part = pl.ds(step * pair, pair)
            wait_for(xk_r.at[rows], xk_recv.at[at])
            wait_for(xv_r.at[rows], xv_recv.at[at])
            dk_s[rows] = (dk_f[part] + xk_r[rows].astype(jnp.float32)).astype(bf16)
            dv_s[rows] = (dv_f[part] + xv_r[rows].astype(jnp.float32)).astype(bf16)
            send_sums(h, step, there)

    steps = members // unroll

    @pl.loop(0, own)
    def _(h):
        for plane in range(2):
            rows = pl.ds(h * docs + half * near + plane * lines, lines)

            @pl.when(jnp.logical_not(is_inner) | ((plane == level) & (h == 0)))
            def _():
                wait_for(k_s.at[rows], k_recv.at[h * 2 + plane])
                wait_for(v_s.at[rows], v_recv.at[h * 2 + plane])

        for plane in range(2):
            rows = pl.ds(h * docs + (1 - half) * near + plane * lines, lines)
            wait_for(k_s.at[rows], kx_recv.at[h * 2 + plane])
            wait_for(v_s.at[rows], vx_recv.at[h * 2 + plane])

        @pl.loop(0, docs)
        def _(d):
            k_tile, v_tile = k_s[h * docs + d], v_s[h * docs + d]
            kn[d] = k_tile
            vn[d] = v_tile
            kt[d] = k_tile.T
            vt[d] = v_tile.T

        here = cols(col * (HEADS // columns) + head_of(h))

        def send_rows(t):
            m = source(t)
            slot = h * members + m

            @pl.when(m == mine)
            def _():
                local(at_s.at[slot], at_out.at[:, here], out_recv.at[0])
                local(dq_s.at[slot], dq_out.at[:, here], out_recv.at[1])

            @pl.when(m != mine)
            def _():
                remote(at_s.at[slot], at_out.at[:, here], out_send.at[0], out_recv.at[0], member(m))
                remote(dq_s.at[slot], dq_out.at[:, here], out_send.at[1], out_recv.at[1], member(m))

        @pl.loop(0, steps)
        def _(step):
            @pl.when(step > 0)
            def _():
                for u in range(unroll):
                    send_rows((step - 1) * unroll + u)

            @pl.when((step == 5) & (h > 0) & (h + 1 < own) & is_inner)
            def _():
                relay(h + 1, 1 - level)

            @pl.when((step == steps - 2) & (h > 0))
            def _():
                finalize(h - 1)

            for u in range(unroll):
                slot = h * members + source(step * unroll + u)
                wait_for(q_s.at[slot], q_recv.at[slot])
                wait_for(do_s.at[slot], do_recv.at[slot])
            f32 = jnp.float32
            which = [source(step * unroll + u) for u in range(unroll)]
            slots = [h * members + m for m in which]
            named = [[spans_ref[seg_ref[half * members + m], j] for j in range(SPANS)] for m in which]
            tops, invs, deltas = [], [], []
            for u in range(unroll):
                k_cat = jnp.concatenate([kn[i] for i in named[u]], axis=0)
                s = lax.dot_general(k_cat, q_s[slots[u]], NT, preferred_element_type=f32)
                s_ref[u] = s
                tops.append(jnp.max(tile_sum(s, jnp.max), axis=0, keepdims=True))
            for u in range(unroll):
                v_cat = jnp.concatenate([vn[i] for i in named[u]], axis=0)
                dp_ref[u] = lax.dot_general(v_cat, do_s[slots[u]], NT, preferred_element_type=f32)
            for u in range(unroll):
                total = jnp.zeros((8, BLOCK), f32)
                mixed = jnp.zeros((8, BLOCK), f32)
                for j in range(SPANS):
                    part = pl.ds(j * BLOCK, BLOCK)
                    e = jnp.exp2((s_ref[u, part] - tops[u]) * (factor * LOG2E))
                    s_ref[u, part] = e
                    total = total + tile_sum(e, jnp.sum)
                    mixed = mixed + tile_sum(e * dp_ref[u, part], jnp.sum)
                inv = 1.0 / jnp.sum(total, axis=0, keepdims=True)
                invs.append(inv)
                deltas.append(jnp.sum(mixed, axis=0, keepdims=True) * inv)
            for u in range(unroll):
                for j in range(SPANS):
                    part = pl.ds(j * BLOCK, BLOCK)
                    p = s_ref[u, part] * invs[u]
                    p_s[which[u], j] = p.astype(bf16)
                    ds_s[which[u], j] = (p * (dp_ref[u, part] - deltas[u])).astype(bf16)
            for u in range(unroll):
                vt_cat = jnp.concatenate([vt[i] for i in named[u]], axis=1)
                kt_cat = jnp.concatenate([kt[i] for i in named[u]], axis=1)
                pb = p_s[which[u], 0:SPANS].reshape(SPANS * BLOCK, BLOCK)
                ds = ds_s[which[u], 0:SPANS].reshape(SPANS * BLOCK, BLOCK)
                attn_t = jnp.dot(vt_cat, pb, preferred_element_type=f32)
                dq_t = jnp.dot(kt_cat, ds, preferred_element_type=f32) * factor
                at_s[slots[u]] = attn_t.T.astype(bf16)
                dq_s[slots[u]] = dq_t.T.astype(bf16)

        for u in range(unroll):
            send_rows(members - unroll + u)

        is_last = h == own - 1
        there = cols(head_of(h))
        beside = cols(line * 2 + jnp.where(is_inner, 0, 1))

        def send_partial(step):
            rows = pl.ds(h * near + step * pair, pair)
            at = h * (near // pair) + step

            @pl.when(jnp.logical_not(is_last))
            def _():
                remote(xk_s.at[rows], xk_r.at[rows], x_send.at[0], xk_recv.at[at], other)
                remote(xv_s.at[rows], xv_r.at[rows], x_send.at[1], xv_recv.at[at], other)

            @pl.when(is_last)
            def _():
                for u in range(pair):
                    slot = h * near + step * pair + u
                    to = ((1 - half) * near + step * pair + u, col)
                    remote(xk_s.at[slot], dk_far.at[:, beside], far_send.at[0], out_recv.at[4], to)
                    remote(xv_s.at[slot], dv_far.at[:, beside], far_send.at[1], out_recv.at[5], to)

        @pl.loop(0, near // pair)
        def _(step):
            @pl.when(step > 0)
            def _():
                send_partial(step - 1)

            rows = pl.ds(h * near + step * pair, pair)
            dk, dv = partial(h, (1 - half) * near + step * pair)
            xk_s[rows] = dk.astype(bf16)
            xv_s[rows] = dv.astype(bf16)

        send_partial(near // pair - 1)

        @pl.loop(0, near // pair)
        def _(step):
            part = pl.ds(step * pair, pair)
            dk, dv = partial(h, half * near + step * pair)

            @pl.when(jnp.logical_not(is_last))
            def _():
                dk_f[part] = dk
                dv_f[part] = dv

            @pl.when(is_last)
            def _():
                rows = pl.ds(h * near + step * pair, pair)
                dk_s[rows] = dk.astype(bf16)
                dv_s[rows] = dv.astype(bf16)
                send_sums(h, step, there)

    outward = sum(1 + a_line % 2 for a_line in range(lines))

    def drain(array, blocks, sem):
        if blocks:
            wait_for(array.at[pl.ds(0, blocks)], sem)

    def drain_sends(count, inside):
        far = outward + (lines if inside else 0)
        for i, array in enumerate((k_s, v_s)):
            drain(array, HEADS // columns - count + far, in_send.at[i])
            drain(array, (2 * count - 1) * lines if inside else 0, relay_send.at[i])
        for i, array in enumerate((q_s, do_s)):
            drain(array, HEADS - count, in_send.at[2 + i])
        for i, array in enumerate((xk_s, xv_s)):
            drain(array, (count - 1) * near, x_send.at[i])
            drain(array, near, far_send.at[i])
        for i, array in enumerate((at_s, dq_s, dk_s, dv_s)):
            drain(array, count * ((members if i < 2 else near) - 1), out_send.at[i])

    for count in range(1, share):
        @pl.when((own == count) & is_inner)
        def _():
            drain_sends(count, True)

        @pl.when((own == count) & jnp.logical_not(is_inner))
        def _():
            drain_sends(count, False)

    for i, array in enumerate((at_s, dq_s, dk_s, dv_s, xk_s, xv_s)):
        drain(array, (HEADS, HEADS // columns, 2 * lines)[i // 2], out_recv.at[i])


def finish_kernel(at_in, dq_in, dk_in, dv_in, dk_far, dv_far, at_ref, dq_ref, dk_ref, dv_ref):
    at_ref[...] = at_in[...]
    dq_ref[...] = dq_in[...]
    pairs = dk_far.shape[1] // (2 * HEAD_DIM)
    share = dk_in.shape[1] // (pairs * HEAD_DIM)
    for src, far, dst in ((dk_in, dk_far, dk_ref), (dv_in, dv_far, dv_ref)):
        for p in range(pairs):
            for j in range(share):
                here = pl.ds((p * share + j) * HEAD_DIM, HEAD_DIM)
                tile = src[:, here]
                inward = share - 1 - p % 2
                if j in (inward - 1, inward):
                    there = pl.ds((p * 2 + j - inward + 1) * HEAD_DIM, HEAD_DIM)
                    total = tile.astype(jnp.float32) + far[:, there].astype(jnp.float32)
                    tile = total.astype(jnp.bfloat16)
                dst[:, here] = tile


def finish(*arrays, steps=2):
    specs = [pl.BlockSpec((a.shape[0], a.shape[1] // steps), lambda i: (0, i)) for a in arrays]
    return pl.pallas_call(
        finish_kernel,
        grid=(steps,),
        out_shape=[jax.ShapeDtypeStruct(a.shape, a.dtype) for a in arrays[:4]],
        in_specs=specs,
        out_specs=specs[:4],
        name="finish",
    )(*arrays)


def body(query, key, value, d_out, seg_map, spans):
    if query.shape[0] != BLOCK or key.shape[0] != BLOCK:
        return body_shared(query, key, value, d_out, seg_map, spans)
    blks, columns = lax.axis_size("blk"), lax.axis_size("head")
    near = blks // 2
    docs, members = blks, near * columns
    most = HEADS // (near // 2 * columns) - 1
    bf16, f32 = jnp.bfloat16, jnp.float32
    dma = pltpu.SemaphoreType.DMA

    def tiles(count, kind=bf16):
        return pltpu.VMEM((count, BLOCK, HEAD_DIM), kind)

    held = pltpu.VMEM((members, SPANS + 1, BLOCK, BLOCK), bf16)
    beside = jax.ShapeDtypeStruct((key.shape[0], near * HEAD_DIM), bf16)
    anywhere = pl.BlockSpec(memory_space=pl.ANY)
    scalars = pl.BlockSpec(memory_space=pltpu.SMEM)
    outs = pl.pallas_call(
        functools.partial(fused_kernel, blks, columns, 1.0 / math.sqrt(HEAD_DIM)),
        out_shape=[jax.ShapeDtypeStruct(a.shape, bf16) for a in (query, query, key, value)] + [beside] * 2,
        in_specs=[scalars] * 2 + [anywhere] * 4,
        out_specs=[anywhere] * 6,
        scratch_shapes=[
            tiles(most * members), tiles(most * members),
            tiles(most * docs), tiles(most * docs),
            tiles(docs), tiles(docs), tiles(docs), tiles(docs),
            held, held,
            tiles(most * members), tiles(most * members),
            tiles(most * near), tiles(most * near),
            tiles(most * near), tiles(most * near),
            tiles(near, f32), tiles(near, f32),
            tiles(most * near), tiles(most * near),
            pltpu.VMEM((2, SPANS * BLOCK, BLOCK), f32), pltpu.VMEM((2, SPANS * BLOCK, BLOCK), f32),
            pltpu.SMEM((spans.shape[0], docs), jnp.int32),
            dma((4,)), dma((2,)), dma((2,)), dma((4,)), dma((2,)),
            dma((most * 2,)), dma((most * 2,)), dma((most * 2,)), dma((most * 2,)),
            dma((most * members,)), dma((most * members,)),
            dma((most * near // 2,)), dma((most * near // 2,)),
            dma((6,)),
        ],
        compiler_params=pltpu.CompilerParams(
            collective_id=0, has_side_effects=True, vmem_limit_bytes=60 << 20
        ),
        name="attend",
    )(seg_map, spans, query, d_out, key, value)
    return finish(*outs)


def fits_one_head_each(mesh):
    return mesh.shape["blk"] * mesh.shape["head"] == HEADS and mesh.shape["blk"] % 8 == 0


def head_pass(q_head, dout_head, key_head, value_head, id_groups):
    factor = 1.0 / math.sqrt(HEAD_DIM)
    group_width = q_head.shape[1]
    doc_blocks = key_head.shape[0]

    def one_group(sums, inputs):
        q_group, dout_group, group_ids = inputs
        flat_ids = group_ids.reshape(group_width * SPANS)
        key_tiles = jnp.take(key_head, flat_ids, axis=0).reshape(
            group_width, SPANS * BLOCK, HEAD_DIM
        )
        value_tiles = jnp.take(value_head, flat_ids, axis=0).reshape(
            group_width, SPANS * BLOCK, HEAD_DIM
        )
        scores = (
            jnp.einsum("cqd,ckd->cqk", q_group, key_tiles, preferred_element_type=jnp.float32)
            * factor
        )
        top_score = jnp.max(scores, axis=-1, keepdims=True)
        expo = jnp.exp(scores - top_score)
        prob = expo / jnp.sum(expo, axis=-1, keepdims=True)
        prob_b = prob.astype(jnp.bfloat16)
        attn = jnp.einsum("cqk,ckd->cqd", prob_b, value_tiles, preferred_element_type=jnp.float32)
        delta = jnp.sum(dout_group.astype(jnp.float32) * attn, axis=-1, keepdims=True)
        dprob = jnp.einsum(
            "cqd,ckd->cqk", dout_group, value_tiles, preferred_element_type=jnp.float32
        )
        dscore_b = (prob * (dprob - delta)).astype(jnp.bfloat16)
        grad_query = (
            jnp.einsum("cqk,ckd->cqd", dscore_b, key_tiles, preferred_element_type=jnp.float32)
            * factor
        ).astype(jnp.bfloat16)
        key_slots = (
            jnp.einsum("cqk,cqd->ckd", dscore_b, q_group, preferred_element_type=jnp.float32)
            * factor
        )
        value_slots = jnp.einsum(
            "cqk,cqd->ckd", prob_b, dout_group, preferred_element_type=jnp.float32
        )
        one_hot = (jnp.arange(doc_blocks, dtype=jnp.int32)[:, None] == flat_ids[None, :]).astype(
            jnp.float32
        )
        key_sums = sums[0] + jnp.dot(
            one_hot,
            key_slots.reshape(group_width * SPANS, BLOCK * HEAD_DIM),
            precision=lax.Precision.HIGHEST,
            preferred_element_type=jnp.float32,
        )
        value_sums = sums[1] + jnp.dot(
            one_hot,
            value_slots.reshape(group_width * SPANS, BLOCK * HEAD_DIM),
            precision=lax.Precision.HIGHEST,
            preferred_element_type=jnp.float32,
        )
        return ((key_sums, value_sums), (attn.astype(jnp.bfloat16), grad_query))

    zero_sums = jnp.zeros((doc_blocks, BLOCK * HEAD_DIM), jnp.float32)
    (key_sums, value_sums), (attn_head, grad_head) = lax.scan(
        one_group, (zero_sums, zero_sums), (q_head, dout_head, id_groups)
    )
    return (attn_head, grad_head, key_sums, value_sums)


def block_table(global_blocks, seg_map, spans):
    block_count = global_blocks.shape[0]
    seg_match = (
        global_blocks[:, None] == jnp.arange(seg_map.shape[0], dtype=jnp.int32)[None, :]
    ).astype(jnp.int32)
    seg_here = jnp.sum(seg_match * seg_map[None, :], axis=1)
    span_match = (seg_here[:, None] == jnp.arange(spans.shape[0], dtype=jnp.int32)[None, :]).astype(
        jnp.int32
    )
    block_ids = jnp.sum(span_match[:, :, None] * spans[None, :, :], axis=1)
    group_width = math.gcd(block_count, max(1, 512 // BLOCK))
    group_count = block_count // group_width
    return (block_ids.reshape(group_count, group_width, SPANS), group_count, group_width)


def by_heads(array, heads_count, group_count, group_width):
    block_count = group_count * group_width
    shaped = array.reshape(block_count, BLOCK, heads_count, HEAD_DIM).transpose(2, 0, 1, 3)
    return shaped.reshape(heads_count, group_count, group_width, BLOCK, HEAD_DIM)


def from_heads(array, heads_count):
    row_count = array.shape[1] * array.shape[2] * BLOCK
    shaped = array.reshape(heads_count, row_count, HEAD_DIM).transpose(1, 0, 2)
    return shaped.reshape(row_count, heads_count * HEAD_DIM)


def from_head_sums(array, heads_count):
    doc_rows = array.shape[1] // HEAD_DIM * BLOCK // BLOCK * array.shape[0] // array.shape[0]
    doc_rows = array.shape[1] * array.shape[2] // (BLOCK * HEAD_DIM) * BLOCK
    shaped = array.reshape(heads_count, doc_rows, HEAD_DIM).transpose(1, 0, 2)
    return shaped.reshape(doc_rows, heads_count * HEAD_DIM)


def body_shared(query, key, value, d_out, seg_map, spans):
    dummy_carry = jnp.zeros((), jnp.int32)
    heads_here = HEADS // lax.axis_size("blk")
    q_rows, dout_rows = (
        lax.all_to_all(query, "blk", split_axis=1, concat_axis=0, tiled=True),
        lax.all_to_all(d_out, "blk", split_axis=1, concat_axis=0, tiled=True),
    )
    per_device = query.shape[0] // BLOCK
    block_count = q_rows.shape[0] // BLOCK
    local_blocks = jnp.arange(block_count, dtype=jnp.int32)
    global_blocks = (
        local_blocks // per_device * lax.axis_size("head") + lax.axis_index("head")
    ) * per_device + local_blocks % per_device
    id_groups, group_count, group_width = block_table(global_blocks, seg_map, spans)
    q_heads = by_heads(q_rows, heads_here, group_count, group_width)
    dout_heads = by_heads(dout_rows, heads_here, group_count, group_width)
    key_wide, value_wide = (
        lax.all_gather(key, "head", axis=1, tiled=True),
        lax.all_gather(value, "head", axis=1, tiled=True),
    )
    key_cols, value_cols = (
        lax.all_to_all(key_wide, "blk", split_axis=1, concat_axis=0, tiled=True),
        lax.all_to_all(value_wide, "blk", split_axis=1, concat_axis=0, tiled=True),
    )
    doc_blocks = key_cols.shape[0] // BLOCK

    def to_blocks(array):
        return array.reshape(doc_blocks, BLOCK, heads_here, HEAD_DIM).transpose(2, 0, 1, 3)

    def scan_head(carry, inputs):
        q_head, dout_head, key_head, value_head = inputs
        return (carry, head_pass(q_head, dout_head, key_head, value_head, id_groups))

    _, (attn_heads, grad_heads, key_parts, value_parts) = lax.scan(
        scan_head, dummy_carry, (q_heads, dout_heads, to_blocks(key_cols), to_blocks(value_cols))
    )
    key_back, value_back = (
        lax.all_to_all(
            from_head_sums(key_parts, heads_here).astype(jnp.bfloat16),
            "blk",
            split_axis=0,
            concat_axis=1,
            tiled=True,
        ).astype(jnp.float32),
        lax.all_to_all(
            from_head_sums(value_parts, heads_here).astype(jnp.bfloat16),
            "blk",
            split_axis=0,
            concat_axis=1,
            tiled=True,
        ).astype(jnp.float32),
    )
    key_total, value_total = (
        lax.psum_scatter(
            key_back.astype(jnp.bfloat16), "head", scatter_dimension=1, tiled=True
        ).astype(jnp.float32),
        lax.psum_scatter(
            value_back.astype(jnp.bfloat16), "head", scatter_dimension=1, tiled=True
        ).astype(jnp.float32),
    )
    attn_out, d_query = (
        lax.all_to_all(
            from_heads(attn_heads, heads_here), "blk", split_axis=0, concat_axis=1, tiled=True
        ),
        lax.all_to_all(
            from_heads(grad_heads, heads_here), "blk", split_axis=0, concat_axis=1, tiled=True
        ),
    )
    return (attn_out, d_query, key_total.astype(jnp.bfloat16), value_total.astype(jnp.bfloat16))


def solution(mesh):
    placed = (
        P(("blk", "head"), None),
        P("blk", "head"),
        P("blk", "head"),
        P(("blk", "head"), None),
        P(),
        P(),
    )
    return jax.shard_map(
        body if fits_one_head_each(mesh) else body_shared,
        mesh=mesh,
        in_specs=placed,
        out_specs=(
            P(("blk", "head"), None),
            P(("blk", "head"), None),
            P("blk", "head"),
            P("blk", "head"),
        ),
        check_vma=False,
    )
```

```python
import functools
import math

import jax
import jax.numpy as jnp
from jax import lax
from jax.experimental import pallas as pl
from jax.experimental.pallas import tpu as pltpu
from jax.sharding import PartitionSpec as P

HEADS = 32
HEAD_DIM = 128
BLOCK = 128
SPANS = 8
LOG2E = math.log2(math.e)

NT = (((1,), (1,)), ((), ()))
MESH = pl.DeviceIdType.MESH


def tile_sum(x, op):
    return op(x.reshape(x.shape[0] // 8, 8, x.shape[1]), axis=0)


def fused_kernel(
    blks, columns, factor,
    seg_ref, spans_ref, q_in, do_in, k_in, v_in,
    at_out, dq_out, dk_out, dv_out, dk_far, dv_far,
    q_s, do_s, k_s, v_s, kn, vn, kt, vt, p_s, ds_s, at_s, dq_s,
    xk_s, xv_s, xk_r, xv_r, dk_f, dv_f, dk_s, dv_s, s_ref, dp_ref, slot_ref,
    in_send, relay_send, x_send, out_send, far_send,
    k_recv, v_recv, kx_recv, vx_recv, q_recv, do_recv, xk_recv, xv_recv, out_recv,
):
    near = blks // 2
    lines = near // 2
    planes = blks // lines
    group = lines * columns
    members = near * columns
    share = HEADS // group
    docs = blks
    unroll, pair, chunk = 2, 4, 8
    blk, col = lax.axis_index("blk"), lax.axis_index("head")
    z, line = blk // lines, lax.rem(blk, lines)
    half = z // 2
    level = z - 2 * half
    place = line * columns + col
    mine = level * group + place
    inner = 1 - half
    is_inner = level == inner

    def inward(a_line):
        return share - 1 - lax.rem(a_line, 2)

    own = jnp.where(is_inner, inward(line), share - inward(line))

    def head_of(h):
        return line * share + jnp.where(is_inner, h, share - 1 - h)

    other = ((planes - 1 - z) * lines + line, col)
    bf16 = jnp.bfloat16

    def cols(index):
        return pl.ds(pl.multiple_of(index * HEAD_DIM, HEAD_DIM), HEAD_DIM)

    def member(m):
        return half * near + m // columns, lax.rem(m, columns)

    def turn(t, size):
        ahead = (t + 1) // 2
        back = lax.rem(t + 1, 2)
        return lax.rem(ahead + back * (size - 2 * ahead) + size, size)

    def local(src, dst, sem):
        pltpu.make_async_copy(src, dst, sem).start()

    def remote(src, dst, send, recv, where):
        pltpu.make_async_remote_copy(
            src_ref=src, dst_ref=dst, send_sem=send, recv_sem=recv,
            device_id=where, device_id_type=MESH,
        ).start()

    def wait_for(view, sem):
        pltpu.make_async_copy(view, view, sem).wait()

    barrier = pltpu.get_barrier_semaphore()

    @pl.loop(0, near)
    def _(t):
        to = ((1 - half) * near + t, col)
        pl.semaphore_signal(barrier, inc=1, device_id=to, device_id_type=MESH)

    @pl.loop(1, members)
    def _(t):
        to = member(lax.rem(mine + t, members))
        pl.semaphore_signal(barrier, inc=1, device_id=to, device_id_type=MESH)

    pl.semaphore_wait(barrier, near + members - 1)

    def place_of(j, to_line):
        inside = j < inward(to_line)
        return jnp.where(inside, inner, 1 - inner), jnp.where(inside, j, share - 1 - j)

    def send_docs(j):
        @pl.loop(0, lines)
        def _(t):
            to_line = lax.rem(line + t, lines)
            to_level, h = place_of(j, to_line)
            slot, at = h * docs + blk, h * 2 + level
            to = half * near + to_level * lines + to_line
            head = cols(to_line * share + j)

            @pl.when(to == blk)
            def _():
                local(k_in.at[:, head], k_s.at[slot], k_recv.at[at])
                local(v_in.at[:, head], v_s.at[slot], v_recv.at[at])

            @pl.when(to != blk)
            def _():
                remote(k_in.at[:, head], k_s.at[slot], in_send.at[0], k_recv.at[at], (to, col))
                remote(v_in.at[:, head], v_s.at[slot], in_send.at[1], v_recv.at[at], (to, col))

    def send_rows_in(j):
        @pl.loop(0, group)
        def _(t):
            spot = lax.rem(place + turn(t, group), group)
            to_line, to_col = spot // columns, lax.rem(spot, columns)
            to_level, h = place_of(j, to_line)
            slot = h * members + mine
            m = to_level * group + spot
            head = cols(to_col * (HEADS // columns) + to_line * share + j)

            @pl.when(m == mine)
            def _():
                local(q_in.at[:, head], q_s.at[slot], q_recv.at[slot])
                local(do_in.at[:, head], do_s.at[slot], do_recv.at[slot])

            @pl.when(m != mine)
            def _():
                remote(q_in.at[:, head], q_s.at[slot], in_send.at[2], q_recv.at[slot], member(m))
                remote(do_in.at[:, head], do_s.at[slot], in_send.at[3], do_recv.at[slot], member(m))

    def send_far(j):
        @pl.loop(0, lines)
        def _(t):
            to_line = lax.rem(line + t, lines)
            h = place_of(j, to_line)[1]
            inside = j < inward(to_line)
            to_z = jnp.where(inside, 2 - half, (planes - 1) * (1 - half))
            slot, at = h * docs + blk, h * 2 + level
            head = cols(to_line * share + j)
            to = (to_z * lines + to_line, col)

            @pl.when(jnp.logical_not(inside) | (is_inner & (j == 0)))
            def _():
                remote(k_in.at[:, head], k_s.at[slot], in_send.at[0], kx_recv.at[at], to)
                remote(v_in.at[:, head], v_s.at[slot], in_send.at[1], vx_recv.at[at], to)

    def relay(h, plane):
        at = h * 2 + plane
        rows = pl.ds(h * docs + half * near + plane * lines, lines)
        wait_for(k_s.at[rows], k_recv.at[at])
        remote(k_s.at[rows], k_s.at[rows], relay_send.at[0], kx_recv.at[at], other)
        wait_for(v_s.at[rows], v_recv.at[at])
        remote(v_s.at[rows], v_s.at[rows], relay_send.at[1], vx_recv.at[at], other)

    last = share - 1
    send_docs(0)

    @pl.when(is_inner)
    def _():
        send_far(0)

    send_docs(1)
    send_docs(last)
    for j in range(2, last):
        send_docs(j)
        send_far(j)
    send_rows_in(0)
    send_rows_in(last)

    @pl.when(is_inner)
    def _():
        relay(0, 1 - level)
        relay(1, level)
        relay(1, 1 - level)

    send_far(last)
    send_rows_in(1)
    for j in range(2, last):
        send_rows_in(j)

    @pl.when(is_inner)
    def _():
        @pl.loop(2, own)
        def _(h):
            relay(h, level)

    @pl.loop(0, spans_ref.shape[0])
    def _(g):
        named = [spans_ref[g, j] for j in range(SPANS)]
        for d in range(docs):
            found = SPANS
            for j in range(SPANS):
                found = jnp.where(named[j] == d, j, found)
            slot_ref[g, d] = found

    @pl.loop(0, members)
    def _(m):
        p_s[m, SPANS] = jnp.zeros((BLOCK, BLOCK), bf16)
        ds_s[m, SPANS] = jnp.zeros((BLOCK, BLOCK), bf16)

    def source(t):
        far = t // group
        spot = lax.rem(place + group - turn(lax.rem(t, group), group), group)
        return lax.rem(level + far, 2) * group + spot

    def partial(h, first):
        ids = [first + u for u in range(pair)]
        outs = []
        for held, right, scale in ((ds_s, q_s, factor), (p_s, do_s, None)):
            total = jnp.zeros((pair * BLOCK, HEAD_DIM), jnp.float32)
            for i in range(0, members, chunk):
                segs = [seg_ref[half * members + i + c] for c in range(chunk)]
                left = jnp.concatenate([
                    jnp.concatenate([held[i + c, slot_ref[segs[c], d]] for c in range(chunk)], axis=1)
                    for d in ids], axis=0)
                rows = right[pl.ds(h * members + i, chunk)].reshape(chunk * BLOCK, HEAD_DIM)
                total = total + jnp.dot(left, rows, preferred_element_type=jnp.float32)
            if scale is not None:
                total = total * scale
            outs.append(total.reshape(pair, BLOCK, HEAD_DIM))
        return outs

    def send_sums(h, step, there):
        for u in range(pair):
            slot = h * near + step * pair + u
            to = half * near + step * pair + u

            @pl.when(to == blk)
            def _():
                local(dk_s.at[slot], dk_out.at[:, there], out_recv.at[2])
                local(dv_s.at[slot], dv_out.at[:, there], out_recv.at[3])

            @pl.when(to != blk)
            def _():
                remote(dk_s.at[slot], dk_out.at[:, there], out_send.at[2], out_recv.at[2], (to, col))
                remote(dv_s.at[slot], dv_out.at[:, there], out_send.at[3], out_recv.at[3], (to, col))

    def finalize(h):
        there = cols(head_of(h))

        @pl.loop(0, near // pair)
        def _(step):
            at = h * (near // pair) + step
            rows = pl.ds(h * near + step * pair, pair)
            part = pl.ds(step * pair, pair)
            wait_for(xk_r.at[rows], xk_recv.at[at])
            wait_for(xv_r.at[rows], xv_recv.at[at])
            dk_s[rows] = (dk_f[part] + xk_r[rows].astype(jnp.float32)).astype(bf16)
            dv_s[rows] = (dv_f[part] + xv_r[rows].astype(jnp.float32)).astype(bf16)
            send_sums(h, step, there)

    steps = members // unroll

    @pl.loop(0, own)
    def _(h):
        for plane in range(2):
            rows = pl.ds(h * docs + half * near + plane * lines, lines)

            @pl.when(jnp.logical_not(is_inner) | ((plane == level) & (h == 0)))
            def _():
                wait_for(k_s.at[rows], k_recv.at[h * 2 + plane])
                wait_for(v_s.at[rows], v_recv.at[h * 2 + plane])

        for plane in range(2):
            rows = pl.ds(h * docs + (1 - half) * near + plane * lines, lines)
            wait_for(k_s.at[rows], kx_recv.at[h * 2 + plane])
            wait_for(v_s.at[rows], vx_recv.at[h * 2 + plane])

        @pl.loop(0, docs)
        def _(d):
            k_tile, v_tile = k_s[h * docs + d], v_s[h * docs + d]
            kn[d] = k_tile
            vn[d] = v_tile
            kt[d] = k_tile.T
            vt[d] = v_tile.T

        here = cols(col * (HEADS // columns) + head_of(h))

        def send_rows(t):
            m = source(t)
            slot = h * members + m

            @pl.when(m == mine)
            def _():
                local(at_s.at[slot], at_out.at[:, here], out_recv.at[0])
                local(dq_s.at[slot], dq_out.at[:, here], out_recv.at[1])

            @pl.when(m != mine)
            def _():
                remote(at_s.at[slot], at_out.at[:, here], out_send.at[0], out_recv.at[0], member(m))
                remote(dq_s.at[slot], dq_out.at[:, here], out_send.at[1], out_recv.at[1], member(m))

        @pl.loop(0, steps)
        def _(step):
            @pl.when(step > 0)
            def _():
                for u in range(unroll):
                    send_rows((step - 1) * unroll + u)

            @pl.when((step == 7) & (h > 0) & (h + 1 < own) & is_inner)
            def _():
                relay(h + 1, 1 - level)

            for u in range(unroll):
                slot = h * members + source(step * unroll + u)
                wait_for(q_s.at[slot], q_recv.at[slot])
                wait_for(do_s.at[slot], do_recv.at[slot])
            f32 = jnp.float32
            which = [source(step * unroll + u) for u in range(unroll)]
            slots = [h * members + m for m in which]
            named = [[spans_ref[seg_ref[half * members + m], j] for j in range(SPANS)] for m in which]
            tops, invs, deltas = [], [], []
            for u in range(unroll):
                k_cat = jnp.concatenate([kn[i] for i in named[u]], axis=0)
                s = lax.dot_general(k_cat, q_s[slots[u]], NT, preferred_element_type=f32)
                s_ref[u] = s
                tops.append(jnp.max(tile_sum(s, jnp.max), axis=0, keepdims=True))
            for u in range(unroll):
                v_cat = jnp.concatenate([vn[i] for i in named[u]], axis=0)
                dp_ref[u] = lax.dot_general(v_cat, do_s[slots[u]], NT, preferred_element_type=f32)
            for u in range(unroll):
                total = jnp.zeros((8, BLOCK), f32)
                mixed = jnp.zeros((8, BLOCK), f32)
                for j in range(SPANS):
                    part = pl.ds(j * BLOCK, BLOCK)
                    e = jnp.exp2((s_ref[u, part] - tops[u]) * (factor * LOG2E))
                    s_ref[u, part] = e
                    total = total + tile_sum(e, jnp.sum)
                    mixed = mixed + tile_sum(e * dp_ref[u, part], jnp.sum)
                inv = 1.0 / jnp.sum(total, axis=0, keepdims=True)
                invs.append(inv)
                deltas.append(jnp.sum(mixed, axis=0, keepdims=True) * inv)
            for u in range(unroll):
                for j in range(SPANS):
                    part = pl.ds(j * BLOCK, BLOCK)
                    p = s_ref[u, part] * invs[u]
                    p_s[which[u], j] = p.astype(bf16)
                    ds_s[which[u], j] = (p * (dp_ref[u, part] - deltas[u])).astype(bf16)
            for u in range(unroll):
                vt_cat = jnp.concatenate([vt[i] for i in named[u]], axis=1)
                kt_cat = jnp.concatenate([kt[i] for i in named[u]], axis=1)
                pb = p_s[which[u], 0:SPANS].reshape(SPANS * BLOCK, BLOCK)
                ds = ds_s[which[u], 0:SPANS].reshape(SPANS * BLOCK, BLOCK)
                attn_t = jnp.dot(vt_cat, pb, preferred_element_type=f32)
                dq_t = jnp.dot(kt_cat, ds, preferred_element_type=f32) * factor
                at_s[slots[u]] = attn_t.T.astype(bf16)
                dq_s[slots[u]] = dq_t.T.astype(bf16)

        for u in range(unroll):
            send_rows(members - unroll + u)

        is_last = h == own - 1
        there = cols(head_of(h))
        beside = cols(line * 2 + jnp.where(is_inner, 0, 1))

        def send_partial(step):
            rows = pl.ds(h * near + step * pair, pair)
            at = h * (near // pair) + step

            @pl.when(jnp.logical_not(is_last))
            def _():
                remote(xk_s.at[rows], xk_r.at[rows], x_send.at[0], xk_recv.at[at], other)
                remote(xv_s.at[rows], xv_r.at[rows], x_send.at[1], xv_recv.at[at], other)

            @pl.when(is_last)
            def _():
                for u in range(pair):
                    slot = h * near + step * pair + u
                    to = ((1 - half) * near + step * pair + u, col)
                    remote(xk_s.at[slot], dk_far.at[:, beside], far_send.at[0], out_recv.at[4], to)
                    remote(xv_s.at[slot], dv_far.at[:, beside], far_send.at[1], out_recv.at[5], to)

        @pl.loop(0, near // pair)
        def _(step):
            @pl.when(step > 0)
            def _():
                send_partial(step - 1)

            rows = pl.ds(h * near + step * pair, pair)
            dk, dv = partial(h, (1 - half) * near + step * pair)
            xk_s[rows] = dk.astype(bf16)
            xv_s[rows] = dv.astype(bf16)

        send_partial(near // pair - 1)

        @pl.when(h > 0)
        def _():
            finalize(h - 1)

        @pl.loop(0, near // pair)
        def _(step):
            part = pl.ds(step * pair, pair)
            dk, dv = partial(h, half * near + step * pair)

            @pl.when(jnp.logical_not(is_last))
            def _():
                dk_f[part] = dk
                dv_f[part] = dv

            @pl.when(is_last)
            def _():
                rows = pl.ds(h * near + step * pair, pair)
                dk_s[rows] = dk.astype(bf16)
                dv_s[rows] = dv.astype(bf16)
                send_sums(h, step, there)

    outward = sum(1 + a_line % 2 for a_line in range(lines))

    def drain(array, blocks, sem):
        if blocks:
            wait_for(array.at[pl.ds(0, blocks)], sem)

    def drain_sends(count, inside):
        far = outward + (lines if inside else 0)
        for i, array in enumerate((k_s, v_s)):
            drain(array, HEADS // columns - count + far, in_send.at[i])
            drain(array, (2 * count - 1) * lines if inside else 0, relay_send.at[i])
        for i, array in enumerate((q_s, do_s)):
            drain(array, HEADS - count, in_send.at[2 + i])
        for i, array in enumerate((xk_s, xv_s)):
            drain(array, (count - 1) * near, x_send.at[i])
            drain(array, near, far_send.at[i])
        for i, array in enumerate((at_s, dq_s, dk_s, dv_s)):
            drain(array, count * ((members if i < 2 else near) - 1), out_send.at[i])

    for count in range(1, share):
        @pl.when((own == count) & is_inner)
        def _():
            drain_sends(count, True)

        @pl.when((own == count) & jnp.logical_not(is_inner))
        def _():
            drain_sends(count, False)

    for i, array in enumerate((at_s, dq_s, dk_s, dv_s, xk_s, xv_s)):
        drain(array, (HEADS, HEADS // columns, 2 * lines)[i // 2], out_recv.at[i])


def finish_kernel(at_in, dq_in, dk_in, dv_in, dk_far, dv_far, at_ref, dq_ref, dk_ref, dv_ref):
    at_ref[...] = at_in[...]
    dq_ref[...] = dq_in[...]
    pairs = dk_far.shape[1] // (2 * HEAD_DIM)
    share = dk_in.shape[1] // (pairs * HEAD_DIM)
    for src, far, dst in ((dk_in, dk_far, dk_ref), (dv_in, dv_far, dv_ref)):
        for p in range(pairs):
            for j in range(share):
                here = pl.ds((p * share + j) * HEAD_DIM, HEAD_DIM)
                tile = src[:, here]
                inward = share - 1 - p % 2
                if j in (inward - 1, inward):
                    there = pl.ds((p * 2 + j - inward + 1) * HEAD_DIM, HEAD_DIM)
                    total = tile.astype(jnp.float32) + far[:, there].astype(jnp.float32)
                    tile = total.astype(jnp.bfloat16)
                dst[:, here] = tile


def finish(*arrays, steps=2):
    specs = [pl.BlockSpec((a.shape[0], a.shape[1] // steps), lambda i: (0, i)) for a in arrays]
    return pl.pallas_call(
        finish_kernel,
        grid=(steps,),
        out_shape=[jax.ShapeDtypeStruct(a.shape, a.dtype) for a in arrays[:4]],
        in_specs=specs,
        out_specs=specs[:4],
        name="finish",
    )(*arrays)


def body(query, key, value, d_out, seg_map, spans):
    if query.shape[0] != BLOCK or key.shape[0] != BLOCK:
        return body_shared(query, key, value, d_out, seg_map, spans)
    blks, columns = lax.axis_size("blk"), lax.axis_size("head")
    near = blks // 2
    docs, members = blks, near * columns
    most = HEADS // (near // 2 * columns) - 1
    bf16, f32 = jnp.bfloat16, jnp.float32
    dma = pltpu.SemaphoreType.DMA

    def tiles(count, kind=bf16):
        return pltpu.VMEM((count, BLOCK, HEAD_DIM), kind)

    held = pltpu.VMEM((members, SPANS + 1, BLOCK, BLOCK), bf16)
    beside = jax.ShapeDtypeStruct((key.shape[0], near * HEAD_DIM), bf16)
    anywhere = pl.BlockSpec(memory_space=pl.ANY)
    scalars = pl.BlockSpec(memory_space=pltpu.SMEM)
    outs = pl.pallas_call(
        functools.partial(fused_kernel, blks, columns, 1.0 / math.sqrt(HEAD_DIM)),
        out_shape=[jax.ShapeDtypeStruct(a.shape, bf16) for a in (query, query, key, value)] + [beside] * 2,
        in_specs=[scalars] * 2 + [anywhere] * 4,
        out_specs=[anywhere] * 6,
        scratch_shapes=[
            tiles(most * members), tiles(most * members),
            tiles(most * docs), tiles(most * docs),
            tiles(docs), tiles(docs), tiles(docs), tiles(docs),
            held, held,
            tiles(most * members), tiles(most * members),
            tiles(most * near), tiles(most * near),
            tiles(most * near), tiles(most * near),
            tiles(near, f32), tiles(near, f32),
            tiles(most * near), tiles(most * near),
            pltpu.VMEM((2, SPANS * BLOCK, BLOCK), f32), pltpu.VMEM((2, SPANS * BLOCK, BLOCK), f32),
            pltpu.SMEM((spans.shape[0], docs), jnp.int32),
            dma((4,)), dma((2,)), dma((2,)), dma((4,)), dma((2,)),
            dma((most * 2,)), dma((most * 2,)), dma((most * 2,)), dma((most * 2,)),
            dma((most * members,)), dma((most * members,)),
            dma((most * near // 4,)), dma((most * near // 4,)),
            dma((6,)),
        ],
        compiler_params=pltpu.CompilerParams(
            collective_id=0, has_side_effects=True, vmem_limit_bytes=60 << 20
        ),
        name="attend",
    )(seg_map, spans, query, d_out, key, value)
    return finish(*outs)


def fits_one_head_each(mesh):
    return mesh.shape["blk"] * mesh.shape["head"] == HEADS and mesh.shape["blk"] % 8 == 0


def head_pass(q_head, dout_head, key_head, value_head, id_groups):
    factor = 1.0 / math.sqrt(HEAD_DIM)
    group_width = q_head.shape[1]
    doc_blocks = key_head.shape[0]

    def one_group(sums, inputs):
        q_group, dout_group, group_ids = inputs
        flat_ids = group_ids.reshape(group_width * SPANS)
        key_tiles = jnp.take(key_head, flat_ids, axis=0).reshape(
            group_width, SPANS * BLOCK, HEAD_DIM
        )
        value_tiles = jnp.take(value_head, flat_ids, axis=0).reshape(
            group_width, SPANS * BLOCK, HEAD_DIM
        )
        scores = (
            jnp.einsum("cqd,ckd->cqk", q_group, key_tiles, preferred_element_type=jnp.float32)
            * factor
        )
        top_score = jnp.max(scores, axis=-1, keepdims=True)
        expo = jnp.exp(scores - top_score)
        prob = expo / jnp.sum(expo, axis=-1, keepdims=True)
        prob_b = prob.astype(jnp.bfloat16)
        attn = jnp.einsum("cqk,ckd->cqd", prob_b, value_tiles, preferred_element_type=jnp.float32)
        delta = jnp.sum(dout_group.astype(jnp.float32) * attn, axis=-1, keepdims=True)
        dprob = jnp.einsum(
            "cqd,ckd->cqk", dout_group, value_tiles, preferred_element_type=jnp.float32
        )
        dscore_b = (prob * (dprob - delta)).astype(jnp.bfloat16)
        grad_query = (
            jnp.einsum("cqk,ckd->cqd", dscore_b, key_tiles, preferred_element_type=jnp.float32)
            * factor
        ).astype(jnp.bfloat16)
        key_slots = (
            jnp.einsum("cqk,cqd->ckd", dscore_b, q_group, preferred_element_type=jnp.float32)
            * factor
        )
        value_slots = jnp.einsum(
            "cqk,cqd->ckd", prob_b, dout_group, preferred_element_type=jnp.float32
        )
        one_hot = (jnp.arange(doc_blocks, dtype=jnp.int32)[:, None] == flat_ids[None, :]).astype(
            jnp.float32
        )
        key_sums = sums[0] + jnp.dot(
            one_hot,
            key_slots.reshape(group_width * SPANS, BLOCK * HEAD_DIM),
            precision=lax.Precision.HIGHEST,
            preferred_element_type=jnp.float32,
        )
        value_sums = sums[1] + jnp.dot(
            one_hot,
            value_slots.reshape(group_width * SPANS, BLOCK * HEAD_DIM),
            precision=lax.Precision.HIGHEST,
            preferred_element_type=jnp.float32,
        )
        return ((key_sums, value_sums), (attn.astype(jnp.bfloat16), grad_query))

    zero_sums = jnp.zeros((doc_blocks, BLOCK * HEAD_DIM), jnp.float32)
    (key_sums, value_sums), (attn_head, grad_head) = lax.scan(
        one_group, (zero_sums, zero_sums), (q_head, dout_head, id_groups)
    )
    return (attn_head, grad_head, key_sums, value_sums)


def block_table(global_blocks, seg_map, spans):
    block_count = global_blocks.shape[0]
    seg_match = (
        global_blocks[:, None] == jnp.arange(seg_map.shape[0], dtype=jnp.int32)[None, :]
    ).astype(jnp.int32)
    seg_here = jnp.sum(seg_match * seg_map[None, :], axis=1)
    span_match = (seg_here[:, None] == jnp.arange(spans.shape[0], dtype=jnp.int32)[None, :]).astype(
        jnp.int32
    )
    block_ids = jnp.sum(span_match[:, :, None] * spans[None, :, :], axis=1)
    group_width = math.gcd(block_count, max(1, 512 // BLOCK))
    group_count = block_count // group_width
    return (block_ids.reshape(group_count, group_width, SPANS), group_count, group_width)


def by_heads(array, heads_count, group_count, group_width):
    block_count = group_count * group_width
    shaped = array.reshape(block_count, BLOCK, heads_count, HEAD_DIM).transpose(2, 0, 1, 3)
    return shaped.reshape(heads_count, group_count, group_width, BLOCK, HEAD_DIM)


def from_heads(array, heads_count):
    row_count = array.shape[1] * array.shape[2] * BLOCK
    shaped = array.reshape(heads_count, row_count, HEAD_DIM).transpose(1, 0, 2)
    return shaped.reshape(row_count, heads_count * HEAD_DIM)


def from_head_sums(array, heads_count):
    doc_rows = array.shape[1] // HEAD_DIM * BLOCK // BLOCK * array.shape[0] // array.shape[0]
    doc_rows = array.shape[1] * array.shape[2] // (BLOCK * HEAD_DIM) * BLOCK
    shaped = array.reshape(heads_count, doc_rows, HEAD_DIM).transpose(1, 0, 2)
    return shaped.reshape(doc_rows, heads_count * HEAD_DIM)


def body_shared(query, key, value, d_out, seg_map, spans):
    dummy_carry = jnp.zeros((), jnp.int32)
    heads_here = HEADS // lax.axis_size("blk")
    q_rows, dout_rows = (
        lax.all_to_all(query, "blk", split_axis=1, concat_axis=0, tiled=True),
        lax.all_to_all(d_out, "blk", split_axis=1, concat_axis=0, tiled=True),
    )
    per_device = query.shape[0] // BLOCK
    block_count = q_rows.shape[0] // BLOCK
    local_blocks = jnp.arange(block_count, dtype=jnp.int32)
    global_blocks = (
        local_blocks // per_device * lax.axis_size("head") + lax.axis_index("head")
    ) * per_device + local_blocks % per_device
    id_groups, group_count, group_width = block_table(global_blocks, seg_map, spans)
    q_heads = by_heads(q_rows, heads_here, group_count, group_width)
    dout_heads = by_heads(dout_rows, heads_here, group_count, group_width)
    key_wide, value_wide = (
        lax.all_gather(key, "head", axis=1, tiled=True),
        lax.all_gather(value, "head", axis=1, tiled=True),
    )
    key_cols, value_cols = (
        lax.all_to_all(key_wide, "blk", split_axis=1, concat_axis=0, tiled=True),
        lax.all_to_all(value_wide, "blk", split_axis=1, concat_axis=0, tiled=True),
    )
    doc_blocks = key_cols.shape[0] // BLOCK

    def to_blocks(array):
        return array.reshape(doc_blocks, BLOCK, heads_here, HEAD_DIM).transpose(2, 0, 1, 3)

    def scan_head(carry, inputs):
        q_head, dout_head, key_head, value_head = inputs
        return (carry, head_pass(q_head, dout_head, key_head, value_head, id_groups))

    _, (attn_heads, grad_heads, key_parts, value_parts) = lax.scan(
        scan_head, dummy_carry, (q_heads, dout_heads, to_blocks(key_cols), to_blocks(value_cols))
    )
    key_back, value_back = (
        lax.all_to_all(
            from_head_sums(key_parts, heads_here).astype(jnp.bfloat16),
            "blk",
            split_axis=0,
            concat_axis=1,
            tiled=True,
        ).astype(jnp.float32),
        lax.all_to_all(
            from_head_sums(value_parts, heads_here).astype(jnp.bfloat16),
            "blk",
            split_axis=0,
            concat_axis=1,
            tiled=True,
        ).astype(jnp.float32),
    )
    key_total, value_total = (
        lax.psum_scatter(
            key_back.astype(jnp.bfloat16), "head", scatter_dimension=1, tiled=True
        ).astype(jnp.float32),
        lax.psum_scatter(
            value_back.astype(jnp.bfloat16), "head", scatter_dimension=1, tiled=True
        ).astype(jnp.float32),
    )
    attn_out, d_query = (
        lax.all_to_all(
            from_heads(attn_heads, heads_here), "blk", split_axis=0, concat_axis=1, tiled=True
        ),
        lax.all_to_all(
            from_heads(grad_heads, heads_here), "blk", split_axis=0, concat_axis=1, tiled=True
        ),
    )
    return (attn_out, d_query, key_total.astype(jnp.bfloat16), value_total.astype(jnp.bfloat16))


def solution(mesh):
    placed = (
        P(("blk", "head"), None),
        P("blk", "head"),
        P("blk", "head"),
        P(("blk", "head"), None),
        P(),
        P(),
    )
    return jax.shard_map(
        body if fits_one_head_each(mesh) else body_shared,
        mesh=mesh,
        in_specs=placed,
        out_specs=(
            P(("blk", "head"), None),
            P(("blk", "head"), None),
            P("blk", "head"),
            P("blk", "head"),
        ),
        check_vma=False,
    )
```

```python
import functools
import math

import jax
import jax.numpy as jnp
from jax import lax
from jax.experimental import pallas as pl
from jax.experimental.pallas import tpu as pltpu
from jax.sharding import PartitionSpec as P

HEADS = 32
HEAD_DIM = 128
BLOCK = 128
SPANS = 8
LOG2E = math.log2(math.e)

NT = (((1,), (1,)), ((), ()))
MESH = pl.DeviceIdType.MESH


def tile_sum(x, op):
    return op(x.reshape(x.shape[0] // 8, 8, x.shape[1]), axis=0)


def fused_kernel(
    blks, columns, factor,
    seg_ref, spans_ref, q_in, do_in, k_in, v_in,
    at_out, dq_out, dk_out, dv_out, dk_far, dv_far,
    q_s, do_s, k_s, v_s, kn, vn, kt, vt, p_s, ds_s, at_s, dq_s,
    xk_s, xv_s, xk_r, xv_r, dk_f, dv_f, dk_s, dv_s, s_ref, dp_ref, slot_ref,
    in_send, relay_send, x_send, out_send, far_send,
    k_recv, v_recv, kx_recv, vx_recv, q_recv, do_recv, xk_recv, xv_recv, out_recv,
):
    near = blks // 2
    lines = near // 2
    planes = blks // lines
    group = lines * columns
    members = near * columns
    share = HEADS // group
    docs = blks
    unroll, pair, chunk = 2, 4, 8
    blk, col = lax.axis_index("blk"), lax.axis_index("head")
    z, line = blk // lines, lax.rem(blk, lines)
    half = z // 2
    level = z - 2 * half
    place = line * columns + col
    mine = level * group + place
    inner = 1 - half
    is_inner = level == inner

    def inward(a_line):
        return share - 1 - lax.rem(a_line, 2)

    own = jnp.where(is_inner, inward(line), share - inward(line))

    def head_of(h):
        return line * share + jnp.where(is_inner, h, share - 1 - h)

    other = ((planes - 1 - z) * lines + line, col)
    bf16 = jnp.bfloat16

    def cols(index):
        return pl.ds(pl.multiple_of(index * HEAD_DIM, HEAD_DIM), HEAD_DIM)

    def member(m):
        return half * near + m // columns, lax.rem(m, columns)

    def turn(t, size):
        ahead = (t + 1) // 2
        back = lax.rem(t + 1, 2)
        return lax.rem(ahead + back * (size - 2 * ahead) + size, size)

    def local(src, dst, sem):
        pltpu.make_async_copy(src, dst, sem).start()

    def remote(src, dst, send, recv, where):
        pltpu.make_async_remote_copy(
            src_ref=src, dst_ref=dst, send_sem=send, recv_sem=recv,
            device_id=where, device_id_type=MESH,
        ).start()

    def wait_for(view, sem):
        pltpu.make_async_copy(view, view, sem).wait()

    barrier = pltpu.get_barrier_semaphore()

    @pl.loop(0, near)
    def _(t):
        to = ((1 - half) * near + t, col)
        pl.semaphore_signal(barrier, inc=1, device_id=to, device_id_type=MESH)

    @pl.loop(1, members)
    def _(t):
        to = member(lax.rem(mine + t, members))
        pl.semaphore_signal(barrier, inc=1, device_id=to, device_id_type=MESH)

    pl.semaphore_wait(barrier, near + members - 1)

    def place_of(j, to_line):
        inside = j < inward(to_line)
        return jnp.where(inside, inner, 1 - inner), jnp.where(inside, j, share - 1 - j)

    def send_docs(j):
        @pl.loop(0, lines)
        def _(t):
            to_line = lax.rem(line + t, lines)
            to_level, h = place_of(j, to_line)
            slot, at = h * docs + blk, h * 2 + level
            to = half * near + to_level * lines + to_line
            head = cols(to_line * share + j)

            @pl.when(to == blk)
            def _():
                local(k_in.at[:, head], k_s.at[slot], k_recv.at[at])
                local(v_in.at[:, head], v_s.at[slot], v_recv.at[at])

            @pl.when(to != blk)
            def _():
                remote(k_in.at[:, head], k_s.at[slot], in_send.at[0], k_recv.at[at], (to, col))
                remote(v_in.at[:, head], v_s.at[slot], in_send.at[1], v_recv.at[at], (to, col))

    def send_rows_in(j):
        @pl.loop(0, group)
        def _(t):
            spot = lax.rem(place + turn(t, group), group)
            to_line, to_col = spot // columns, lax.rem(spot, columns)
            to_level, h = place_of(j, to_line)
            slot = h * members + mine
            m = to_level * group + spot
            head = cols(to_col * (HEADS // columns) + to_line * share + j)

            @pl.when(m == mine)
            def _():
                local(q_in.at[:, head], q_s.at[slot], q_recv.at[slot])
                local(do_in.at[:, head], do_s.at[slot], do_recv.at[slot])

            @pl.when(m != mine)
            def _():
                remote(q_in.at[:, head], q_s.at[slot], in_send.at[2], q_recv.at[slot], member(m))
                remote(do_in.at[:, head], do_s.at[slot], in_send.at[3], do_recv.at[slot], member(m))

    def send_far(j):
        @pl.loop(0, lines)
        def _(t):
            to_line = lax.rem(line + t, lines)
            h = place_of(j, to_line)[1]
            inside = j < inward(to_line)
            to_z = jnp.where(inside, 2 - half, (planes - 1) * (1 - half))
            slot, at = h * docs + blk, h * 2 + level
            head = cols(to_line * share + j)
            to = (to_z * lines + to_line, col)

            @pl.when(jnp.logical_not(inside) | (is_inner & (j == 0)))
            def _():
                remote(k_in.at[:, head], k_s.at[slot], in_send.at[0], kx_recv.at[at], to)
                remote(v_in.at[:, head], v_s.at[slot], in_send.at[1], vx_recv.at[at], to)

    def relay(h, plane):
        at = h * 2 + plane
        rows = pl.ds(h * docs + half * near + plane * lines, lines)
        wait_for(k_s.at[rows], k_recv.at[at])
        remote(k_s.at[rows], k_s.at[rows], relay_send.at[0], kx_recv.at[at], other)
        wait_for(v_s.at[rows], v_recv.at[at])
        remote(v_s.at[rows], v_s.at[rows], relay_send.at[1], vx_recv.at[at], other)

    last = share - 1
    send_docs(0)

    @pl.when(is_inner)
    def _():
        send_far(0)

    send_docs(1)
    send_docs(last)
    for j in range(2, last):
        send_docs(j)
        send_far(j)
    send_rows_in(0)
    send_rows_in(last)

    @pl.when(is_inner)
    def _():
        relay(0, 1 - level)
        relay(1, level)
        relay(1, 1 - level)

    send_far(last)
    send_rows_in(1)
    for j in range(2, last):
        send_rows_in(j)

    @pl.when(is_inner)
    def _():
        @pl.loop(2, own)
        def _(h):
            relay(h, level)

    @pl.loop(0, spans_ref.shape[0])
    def _(g):
        named = [spans_ref[g, j] for j in range(SPANS)]
        for d in range(docs):
            found = SPANS
            for j in range(SPANS):
                found = jnp.where(named[j] == d, j, found)
            slot_ref[g, d] = found

    @pl.loop(0, members)
    def _(m):
        p_s[m, SPANS] = jnp.zeros((BLOCK, BLOCK), bf16)
        ds_s[m, SPANS] = jnp.zeros((BLOCK, BLOCK), bf16)

    def source(t):
        far = t // group
        spot = lax.rem(place + group - turn(lax.rem(t, group), group), group)
        return lax.rem(level + far, 2) * group + spot

    def partial(h, first):
        ids = [first + u for u in range(pair)]
        outs = []
        for held, right, scale in ((ds_s, q_s, factor), (p_s, do_s, None)):
            total = jnp.zeros((pair * BLOCK, HEAD_DIM), jnp.float32)
            for i in range(0, members, chunk):
                segs = [seg_ref[half * members + i + c] for c in range(chunk)]
                left = jnp.concatenate([
                    jnp.concatenate([held[i + c, slot_ref[segs[c], d]] for c in range(chunk)], axis=1)
                    for d in ids], axis=0)
                rows = right[pl.ds(h * members + i, chunk)].reshape(chunk * BLOCK, HEAD_DIM)
                total = total + jnp.dot(left, rows, preferred_element_type=jnp.float32)
            if scale is not None:
                total = total * scale
            outs.append(total.reshape(pair, BLOCK, HEAD_DIM))
        return outs

    def send_sums(h, step, there):
        for u in range(pair):
            slot = h * near + step * pair + u
            to = half * near + step * pair + u

            @pl.when(to == blk)
            def _():
                local(dk_s.at[slot], dk_out.at[:, there], out_recv.at[2])
                local(dv_s.at[slot], dv_out.at[:, there], out_recv.at[3])

            @pl.when(to != blk)
            def _():
                remote(dk_s.at[slot], dk_out.at[:, there], out_send.at[2], out_recv.at[2], (to, col))
                remote(dv_s.at[slot], dv_out.at[:, there], out_send.at[3], out_recv.at[3], (to, col))

    def finalize(h):
        there = cols(head_of(h))

        @pl.loop(0, near // pair)
        def _(step):
            at = h * (near // pair) + step
            rows = pl.ds(h * near + step * pair, pair)
            part = pl.ds(step * pair, pair)
            wait_for(xk_r.at[rows], xk_recv.at[at])
            wait_for(xv_r.at[rows], xv_recv.at[at])
            dk_s[rows] = (dk_f[part] + xk_r[rows].astype(jnp.float32)).astype(bf16)
            dv_s[rows] = (dv_f[part] + xv_r[rows].astype(jnp.float32)).astype(bf16)
            send_sums(h, step, there)

    steps = members // unroll

    @pl.loop(0, own)
    def _(h):
        for plane in range(2):
            rows = pl.ds(h * docs + half * near + plane * lines, lines)

            @pl.when(jnp.logical_not(is_inner) | ((plane == level) & (h == 0)))
            def _():
                wait_for(k_s.at[rows], k_recv.at[h * 2 + plane])
                wait_for(v_s.at[rows], v_recv.at[h * 2 + plane])

        for plane in range(2):
            rows = pl.ds(h * docs + (1 - half) * near + plane * lines, lines)
            wait_for(k_s.at[rows], kx_recv.at[h * 2 + plane])
            wait_for(v_s.at[rows], vx_recv.at[h * 2 + plane])

        @pl.loop(0, docs)
        def _(d):
            k_tile, v_tile = k_s[h * docs + d], v_s[h * docs + d]
            kn[d] = k_tile
            vn[d] = v_tile
            kt[d] = k_tile.T
            vt[d] = v_tile.T

        here = cols(col * (HEADS // columns) + head_of(h))

        def send_rows(t):
            m = source(t)
            slot = h * members + m

            @pl.when(m == mine)
            def _():
                local(at_s.at[slot], at_out.at[:, here], out_recv.at[0])
                local(dq_s.at[slot], dq_out.at[:, here], out_recv.at[1])

            @pl.when(m != mine)
            def _():
                remote(at_s.at[slot], at_out.at[:, here], out_send.at[0], out_recv.at[0], member(m))
                remote(dq_s.at[slot], dq_out.at[:, here], out_send.at[1], out_recv.at[1], member(m))

        @pl.loop(0, steps)
        def _(step):
            @pl.when(step > 0)
            def _():
                for u in range(unroll):
                    send_rows((step - 1) * unroll + u)

            @pl.when((step == 2) & (h == 0) & is_inner)
            def _():
                @pl.loop(2, own)
                def _(later):
                    relay(later, 1 - level)

            for u in range(unroll):
                slot = h * members + source(step * unroll + u)
                wait_for(q_s.at[slot], q_recv.at[slot])
                wait_for(do_s.at[slot], do_recv.at[slot])
            f32 = jnp.float32
            which = [source(step * unroll + u) for u in range(unroll)]
            slots = [h * members + m for m in which]
            named = [[spans_ref[seg_ref[half * members + m], j] for j in range(SPANS)] for m in which]
            tops, invs, deltas = [], [], []
            for u in range(unroll):
                k_cat = jnp.concatenate([kn[i] for i in named[u]], axis=0)
                s = lax.dot_general(k_cat, q_s[slots[u]], NT, preferred_element_type=f32)
                s_ref[u] = s
                tops.append(jnp.max(tile_sum(s, jnp.max), axis=0, keepdims=True))
            for u in range(unroll):
                v_cat = jnp.concatenate([vn[i] for i in named[u]], axis=0)
                dp_ref[u] = lax.dot_general(v_cat, do_s[slots[u]], NT, preferred_element_type=f32)
            for u in range(unroll):
                total = jnp.zeros((8, BLOCK), f32)
                mixed = jnp.zeros((8, BLOCK), f32)
                for j in range(SPANS):
                    part = pl.ds(j * BLOCK, BLOCK)
                    e = jnp.exp2((s_ref[u, part] - tops[u]) * (factor * LOG2E))
                    s_ref[u, part] = e
                    total = total + tile_sum(e, jnp.sum)
                    mixed = mixed + tile_sum(e * dp_ref[u, part], jnp.sum)
                inv = 1.0 / jnp.sum(total, axis=0, keepdims=True)
                invs.append(inv)
                deltas.append(jnp.sum(mixed, axis=0, keepdims=True) * inv)
            for u in range(unroll):
                for j in range(SPANS):
                    part = pl.ds(j * BLOCK, BLOCK)
                    p = s_ref[u, part] * invs[u]
                    p_s[which[u], j] = p.astype(bf16)
                    ds_s[which[u], j] = (p * (dp_ref[u, part] - deltas[u])).astype(bf16)
            for u in range(unroll):
                vt_cat = jnp.concatenate([vt[i] for i in named[u]], axis=1)
                kt_cat = jnp.concatenate([kt[i] for i in named[u]], axis=1)
                pb = p_s[which[u], 0:SPANS].reshape(SPANS * BLOCK, BLOCK)
                ds = ds_s[which[u], 0:SPANS].reshape(SPANS * BLOCK, BLOCK)
                attn_t = jnp.dot(vt_cat, pb, preferred_element_type=f32)
                dq_t = jnp.dot(kt_cat, ds, preferred_element_type=f32) * factor
                at_s[slots[u]] = attn_t.T.astype(bf16)
                dq_s[slots[u]] = dq_t.T.astype(bf16)

        for u in range(unroll):
            send_rows(members - unroll + u)

        is_last = h == own - 1
        there = cols(head_of(h))
        beside = cols(line * 2 + jnp.where(is_inner, 0, 1))

        def send_partial(step):
            rows = pl.ds(h * near + step * pair, pair)
            at = h * (near // pair) + step

            @pl.when(jnp.logical_not(is_last))
            def _():
                remote(xk_s.at[rows], xk_r.at[rows], x_send.at[0], xk_recv.at[at], other)
                remote(xv_s.at[rows], xv_r.at[rows], x_send.at[1], xv_recv.at[at], other)

            @pl.when(is_last)
            def _():
                for u in range(pair):
                    slot = h * near + step * pair + u
                    to = ((1 - half) * near + step * pair + u, col)
                    remote(xk_s.at[slot], dk_far.at[:, beside], far_send.at[0], out_recv.at[4], to)
                    remote(xv_s.at[slot], dv_far.at[:, beside], far_send.at[1], out_recv.at[5], to)

        @pl.loop(0, near // pair)
        def _(step):
            @pl.when(step > 0)
            def _():
                send_partial(step - 1)

            rows = pl.ds(h * near + step * pair, pair)
            dk, dv = partial(h, (1 - half) * near + step * pair)
            xk_s[rows] = dk.astype(bf16)
            xv_s[rows] = dv.astype(bf16)

        send_partial(near // pair - 1)

        @pl.when(h > 0)
        def _():
            finalize(h - 1)

        @pl.loop(0, near // pair)
        def _(step):
            part = pl.ds(step * pair, pair)
            dk, dv = partial(h, half * near + step * pair)

            @pl.when(jnp.logical_not(is_last))
            def _():
                dk_f[part] = dk
                dv_f[part] = dv

            @pl.when(is_last)
            def _():
                rows = pl.ds(h * near + step * pair, pair)
                dk_s[rows] = dk.astype(bf16)
                dv_s[rows] = dv.astype(bf16)
                send_sums(h, step, there)

    outward = sum(1 + a_line % 2 for a_line in range(lines))

    def drain(array, blocks, sem):
        if blocks:
            wait_for(array.at[pl.ds(0, blocks)], sem)

    def drain_sends(count, inside):
        far = outward + (lines if inside else 0)
        for i, array in enumerate((k_s, v_s)):
            drain(array, HEADS // columns - count + far, in_send.at[i])
            drain(array, (2 * count - 1) * lines if inside else 0, relay_send.at[i])
        for i, array in enumerate((q_s, do_s)):
            drain(array, HEADS - count, in_send.at[2 + i])
        for i, array in enumerate((xk_s, xv_s)):
            drain(array, (count - 1) * near, x_send.at[i])
            drain(array, near, far_send.at[i])
        for i, array in enumerate((at_s, dq_s, dk_s, dv_s)):
            drain(array, count * ((members if i < 2 else near) - 1), out_send.at[i])

    for count in range(1, share):
        @pl.when((own == count) & is_inner)
        def _():
            drain_sends(count, True)

        @pl.when((own == count) & jnp.logical_not(is_inner))
        def _():
            drain_sends(count, False)

    for i, array in enumerate((at_s, dq_s, dk_s, dv_s, xk_s, xv_s)):
        drain(array, (HEADS, HEADS // columns, 2 * lines)[i // 2], out_recv.at[i])


def finish_kernel(at_in, dq_in, dk_in, dv_in, dk_far, dv_far, at_ref, dq_ref, dk_ref, dv_ref):
    at_ref[...] = at_in[...]
    dq_ref[...] = dq_in[...]
    pairs = dk_far.shape[1] // (2 * HEAD_DIM)
    share = dk_in.shape[1] // (pairs * HEAD_DIM)
    for src, far, dst in ((dk_in, dk_far, dk_ref), (dv_in, dv_far, dv_ref)):
        for p in range(pairs):
            for j in range(share):
                here = pl.ds((p * share + j) * HEAD_DIM, HEAD_DIM)
                tile = src[:, here]
                inward = share - 1 - p % 2
                if j in (inward - 1, inward):
                    there = pl.ds((p * 2 + j - inward + 1) * HEAD_DIM, HEAD_DIM)
                    total = tile.astype(jnp.float32) + far[:, there].astype(jnp.float32)
                    tile = total.astype(jnp.bfloat16)
                dst[:, here] = tile


def finish(*arrays, steps=2):
    specs = [pl.BlockSpec((a.shape[0], a.shape[1] // steps), lambda i: (0, i)) for a in arrays]
    return pl.pallas_call(
        finish_kernel,
        grid=(steps,),
        out_shape=[jax.ShapeDtypeStruct(a.shape, a.dtype) for a in arrays[:4]],
        in_specs=specs,
        out_specs=specs[:4],
        name="finish",
    )(*arrays)


def body(query, key, value, d_out, seg_map, spans):
    if query.shape[0] != BLOCK or key.shape[0] != BLOCK:
        return body_shared(query, key, value, d_out, seg_map, spans)
    blks, columns = lax.axis_size("blk"), lax.axis_size("head")
    near = blks // 2
    docs, members = blks, near * columns
    most = HEADS // (near // 2 * columns) - 1
    bf16, f32 = jnp.bfloat16, jnp.float32
    dma = pltpu.SemaphoreType.DMA

    def tiles(count, kind=bf16):
        return pltpu.VMEM((count, BLOCK, HEAD_DIM), kind)

    held = pltpu.VMEM((members, SPANS + 1, BLOCK, BLOCK), bf16)
    beside = jax.ShapeDtypeStruct((key.shape[0], near * HEAD_DIM), bf16)
    anywhere = pl.BlockSpec(memory_space=pl.ANY)
    scalars = pl.BlockSpec(memory_space=pltpu.SMEM)
    outs = pl.pallas_call(
        functools.partial(fused_kernel, blks, columns, 1.0 / math.sqrt(HEAD_DIM)),
        out_shape=[jax.ShapeDtypeStruct(a.shape, bf16) for a in (query, query, key, value)] + [beside] * 2,
        in_specs=[scalars] * 2 + [anywhere] * 4,
        out_specs=[anywhere] * 6,
        scratch_shapes=[
            tiles(most * members), tiles(most * members),
            tiles(most * docs), tiles(most * docs),
            tiles(docs), tiles(docs), tiles(docs), tiles(docs),
            held, held,
            tiles(most * members), tiles(most * members),
            tiles(most * near), tiles(most * near),
            tiles(most * near), tiles(most * near),
            tiles(near, f32), tiles(near, f32),
            tiles(most * near), tiles(most * near),
            pltpu.VMEM((2, SPANS * BLOCK, BLOCK), f32), pltpu.VMEM((2, SPANS * BLOCK, BLOCK), f32),
            pltpu.SMEM((spans.shape[0], docs), jnp.int32),
            dma((4,)), dma((2,)), dma((2,)), dma((4,)), dma((2,)),
            dma((most * 2,)), dma((most * 2,)), dma((most * 2,)), dma((most * 2,)),
            dma((most * members,)), dma((most * members,)),
            dma((most * near // 4,)), dma((most * near // 4,)),
            dma((6,)),
        ],
        compiler_params=pltpu.CompilerParams(
            collective_id=0, has_side_effects=True, vmem_limit_bytes=60 << 20
        ),
        name="attend",
    )(seg_map, spans, query, d_out, key, value)
    return finish(*outs)


def fits_one_head_each(mesh):
    return mesh.shape["blk"] * mesh.shape["head"] == HEADS and mesh.shape["blk"] % 8 == 0


def head_pass(q_head, dout_head, key_head, value_head, id_groups):
    factor = 1.0 / math.sqrt(HEAD_DIM)
    group_width = q_head.shape[1]
    doc_blocks = key_head.shape[0]

    def one_group(sums, inputs):
        q_group, dout_group, group_ids = inputs
        flat_ids = group_ids.reshape(group_width * SPANS)
        key_tiles = jnp.take(key_head, flat_ids, axis=0).reshape(
            group_width, SPANS * BLOCK, HEAD_DIM
        )
        value_tiles = jnp.take(value_head, flat_ids, axis=0).reshape(
            group_width, SPANS * BLOCK, HEAD_DIM
        )
        scores = (
            jnp.einsum("cqd,ckd->cqk", q_group, key_tiles, preferred_element_type=jnp.float32)
            * factor
        )
        top_score = jnp.max(scores, axis=-1, keepdims=True)
        expo = jnp.exp(scores - top_score)
        prob = expo / jnp.sum(expo, axis=-1, keepdims=True)
        prob_b = prob.astype(jnp.bfloat16)
        attn = jnp.einsum("cqk,ckd->cqd", prob_b, value_tiles, preferred_element_type=jnp.float32)
        delta = jnp.sum(dout_group.astype(jnp.float32) * attn, axis=-1, keepdims=True)
        dprob = jnp.einsum(
            "cqd,ckd->cqk", dout_group, value_tiles, preferred_element_type=jnp.float32
        )
        dscore_b = (prob * (dprob - delta)).astype(jnp.bfloat16)
        grad_query = (
            jnp.einsum("cqk,ckd->cqd", dscore_b, key_tiles, preferred_element_type=jnp.float32)
            * factor
        ).astype(jnp.bfloat16)
        key_slots = (
            jnp.einsum("cqk,cqd->ckd", dscore_b, q_group, preferred_element_type=jnp.float32)
            * factor
        )
        value_slots = jnp.einsum(
            "cqk,cqd->ckd", prob_b, dout_group, preferred_element_type=jnp.float32
        )
        one_hot = (jnp.arange(doc_blocks, dtype=jnp.int32)[:, None] == flat_ids[None, :]).astype(
            jnp.float32
        )
        key_sums = sums[0] + jnp.dot(
            one_hot,
            key_slots.reshape(group_width * SPANS, BLOCK * HEAD_DIM),
            precision=lax.Precision.HIGHEST,
            preferred_element_type=jnp.float32,
        )
        value_sums = sums[1] + jnp.dot(
            one_hot,
            value_slots.reshape(group_width * SPANS, BLOCK * HEAD_DIM),
            precision=lax.Precision.HIGHEST,
            preferred_element_type=jnp.float32,
        )
        return ((key_sums, value_sums), (attn.astype(jnp.bfloat16), grad_query))

    zero_sums = jnp.zeros((doc_blocks, BLOCK * HEAD_DIM), jnp.float32)
    (key_sums, value_sums), (attn_head, grad_head) = lax.scan(
        one_group, (zero_sums, zero_sums), (q_head, dout_head, id_groups)
    )
    return (attn_head, grad_head, key_sums, value_sums)


def block_table(global_blocks, seg_map, spans):
    block_count = global_blocks.shape[0]
    seg_match = (
        global_blocks[:, None] == jnp.arange(seg_map.shape[0], dtype=jnp.int32)[None, :]
    ).astype(jnp.int32)
    seg_here = jnp.sum(seg_match * seg_map[None, :], axis=1)
    span_match = (seg_here[:, None] == jnp.arange(spans.shape[0], dtype=jnp.int32)[None, :]).astype(
        jnp.int32
    )
    block_ids = jnp.sum(span_match[:, :, None] * spans[None, :, :], axis=1)
    group_width = math.gcd(block_count, max(1, 512 // BLOCK))
    group_count = block_count // group_width
    return (block_ids.reshape(group_count, group_width, SPANS), group_count, group_width)


def by_heads(array, heads_count, group_count, group_width):
    block_count = group_count * group_width
    shaped = array.reshape(block_count, BLOCK, heads_count, HEAD_DIM).transpose(2, 0, 1, 3)
    return shaped.reshape(heads_count, group_count, group_width, BLOCK, HEAD_DIM)


def from_heads(array, heads_count):
    row_count = array.shape[1] * array.shape[2] * BLOCK
    shaped = array.reshape(heads_count, row_count, HEAD_DIM).transpose(1, 0, 2)
    return shaped.reshape(row_count, heads_count * HEAD_DIM)


def from_head_sums(array, heads_count):
    doc_rows = array.shape[1] // HEAD_DIM * BLOCK // BLOCK * array.shape[0] // array.shape[0]
    doc_rows = array.shape[1] * array.shape[2] // (BLOCK * HEAD_DIM) * BLOCK
    shaped = array.reshape(heads_count, doc_rows, HEAD_DIM).transpose(1, 0, 2)
    return shaped.reshape(doc_rows, heads_count * HEAD_DIM)


def body_shared(query, key, value, d_out, seg_map, spans):
    dummy_carry = jnp.zeros((), jnp.int32)
    heads_here = HEADS // lax.axis_size("blk")
    q_rows, dout_rows = (
        lax.all_to_all(query, "blk", split_axis=1, concat_axis=0, tiled=True),
        lax.all_to_all(d_out, "blk", split_axis=1, concat_axis=0, tiled=True),
    )
    per_device = query.shape[0] // BLOCK
    block_count = q_rows.shape[0] // BLOCK
    local_blocks = jnp.arange(block_count, dtype=jnp.int32)
    global_blocks = (
        local_blocks // per_device * lax.axis_size("head") + lax.axis_index("head")
    ) * per_device + local_blocks % per_device
    id_groups, group_count, group_width = block_table(global_blocks, seg_map, spans)
    q_heads = by_heads(q_rows, heads_here, group_count, group_width)
    dout_heads = by_heads(dout_rows, heads_here, group_count, group_width)
    key_wide, value_wide = (
        lax.all_gather(key, "head", axis=1, tiled=True),
        lax.all_gather(value, "head", axis=1, tiled=True),
    )
    key_cols, value_cols = (
        lax.all_to_all(key_wide, "blk", split_axis=1, concat_axis=0, tiled=True),
        lax.all_to_all(value_wide, "blk", split_axis=1, concat_axis=0, tiled=True),
    )
    doc_blocks = key_cols.shape[0] // BLOCK

    def to_blocks(array):
        return array.reshape(doc_blocks, BLOCK, heads_here, HEAD_DIM).transpose(2, 0, 1, 3)

    def scan_head(carry, inputs):
        q_head, dout_head, key_head, value_head = inputs
        return (carry, head_pass(q_head, dout_head, key_head, value_head, id_groups))

    _, (attn_heads, grad_heads, key_parts, value_parts) = lax.scan(
        scan_head, dummy_carry, (q_heads, dout_heads, to_blocks(key_cols), to_blocks(value_cols))
    )
    key_back, value_back = (
        lax.all_to_all(
            from_head_sums(key_parts, heads_here).astype(jnp.bfloat16),
            "blk",
            split_axis=0,
            concat_axis=1,
            tiled=True,
        ).astype(jnp.float32),
        lax.all_to_all(
            from_head_sums(value_parts, heads_here).astype(jnp.bfloat16),
            "blk",
            split_axis=0,
            concat_axis=1,
            tiled=True,
        ).astype(jnp.float32),
    )
    key_total, value_total = (
        lax.psum_scatter(
            key_back.astype(jnp.bfloat16), "head", scatter_dimension=1, tiled=True
        ).astype(jnp.float32),
        lax.psum_scatter(
            value_back.astype(jnp.bfloat16), "head", scatter_dimension=1, tiled=True
        ).astype(jnp.float32),
    )
    attn_out, d_query = (
        lax.all_to_all(
            from_heads(attn_heads, heads_here), "blk", split_axis=0, concat_axis=1, tiled=True
        ),
        lax.all_to_all(
            from_heads(grad_heads, heads_here), "blk", split_axis=0, concat_axis=1, tiled=True
        ),
    )
    return (attn_out, d_query, key_total.astype(jnp.bfloat16), value_total.astype(jnp.bfloat16))


def solution(mesh):
    placed = (
        P(("blk", "head"), None),
        P("blk", "head"),
        P("blk", "head"),
        P(("blk", "head"), None),
        P(),
        P(),
    )
    return jax.shard_map(
        body if fits_one_head_each(mesh) else body_shared,
        mesh=mesh,
        in_specs=placed,
        out_specs=(
            P(("blk", "head"), None),
            P(("blk", "head"), None),
            P("blk", "head"),
            P("blk", "head"),
        ),
        check_vma=False,
    )
```
